128 devices in a mesh: dp: 16 (over y, x), mp: 8 (over z, core).
Axes of the slice: x: 4, y: 4, z: 4, core: 2. Of those that a mesh axis runs over, the one named last changes fastest.
Arguments:
- tokens: bfloat16 [8192, 4096], P('dp'), may hold values from -6 to 6
- cache: bfloat16 [384, 128, 896], P('dp'), may hold values from -220 to 220
- nb_row: int32 [128, 2], P('dp'), may hold values from 0 to 23
- nb_owner: int32 [128, 2], P('dp'), may hold values from 0 to 15, all different within a row; in each aligned block of 8 rows (0 to 7, 8 to 15, ...) at most 3 rows name the same one
- nb_len: int32 [128, 2], P('dp'), may hold values from 32 to 128, as said below
- w_query: bfloat16 [4096, 4096], P('dp', 'mp'), may hold values from -0.09375 to 0.09375
- w_key: bfloat16 [896, 4096], P('dp', 'mp'), may hold values from -0.1875 to 0.1875
- w_value: bfloat16 [896, 4096], P('dp', 'mp'), may hold values from -0.1875 to 0.1875
- w_out: bfloat16 [4096, 4096], P('mp', 'dp'), may hold values from -0.09375 to 0.09375
- grad_out: bfloat16 [8192, 4096], P('dp'), may hold values from -6 to 6
Outputs:
- mixed: bfloat16 [8192, 4096], P('dp', 'mp')
- grad_tokens: bfloat16 [8192, 4096], P('dp', 'mp')
- grad_query: float32 [4096, 4096], P('dp', 'mp')
- grad_key: float32 [896, 4096], P('dp', 'mp')
- grad_value: float32 [896, 4096], P('dp', 'mp')
- grad_wout: float32 [4096, 4096], P('mp', 'dp')
The draws below stay inside these ranges and needn't reach their ends.
Inputs may be any that keep to these rules, and one draw needn't show every extreme that they name: `nb_owner`: among the 8 stretches of one index of dp no shard is named more than 3 times, a bound that some block reaches; the 2 neighbours of a stretch lie on different shards. `nb_len`: the first neighbour of every stretch has all 128 tokens.
All inputs are finite; a program needn't handle non-finite values.
Results may differ from the reference program's by a relative error of at most 0.014.
The reference program's roundings to bfloat16 on the way (of `normed`, `queries`, `blocks`, `prob`, `attended`, `grad_attn` and `grad_scores`) count: a program that leaves them out, or rounds other values in their place, can miss the bound.
Values may be sent and summed in bfloat16 or wider, within the bound.
No kernel may reach another device: no remote copies, remote signals or barrier semaphores. Data moves between devices by JAX's collectives and lax.ppermute only.
A program may use at most 128 MiB of HBM per device.

```python
import math
import jax
import jax.numpy as jnp
import numpy as np
from jax import lax

D = 4096
HEADS = 32
HD = 128
ENC = 896
CL = 64
KN = 2
NL = 128
CAP = 3
DB_DEV = 24
STRETCH_DEV = 8
TOKENS = 8192
STRETCHES = 128
DBCHUNKS = 384
N_DP = 16
N_MP = 8


def draw_cache(key, part):
    base = jnp.clip(jax.random.normal(key, (DBCHUNKS, NL, ENC), jnp.float32), -6.0, 6.0)
    return base.astype(jnp.bfloat16)


def draw_nb_len(key, part):
    first_len = jnp.full((STRETCHES, 1), NL, jnp.int32)
    others = jax.random.randint(jax.random.fold_in(key, 3), (STRETCHES, KN - 1), NL // 4, NL + 1).astype(jnp.int32)
    return jnp.concatenate([first_len, others], axis=1)


def place_ends(array, rng, low, high):
    extent = array.shape
    index_at = [jax.random.randint(jax.random.fold_in(rng, axis), (), 0, extent[axis]) for axis in range(len(extent))]
    array = array.at[tuple(index_at)].set(low)
    longest = extent.index(max(extent))
    index_at[longest] = (index_at[longest] + 1) % extent[longest]
    return array.at[tuple(index_at)].set(high)


def with_spikes(result, key, source, target, shards_of, factor):
    def block_of(axis_at):
        return (jnp.arange(result.shape[axis_at]) // (result.shape[axis_at] // shards_of)).reshape((-1,) + (1,) * (result.ndim - 1 - axis_at))

    near = jax.random.permutation(key, shards_of)[block_of(target)]
    second = (block_of(target) + shards_of // 2) % shards_of
    return jnp.where((block_of(source) == near) | (block_of(source) == second), factor * result, result)


def shard_levels(stream_key, shape, split, low, high):
    loudness = 1.0
    for axis_at, parts in split:
        steps = jax.random.uniform(jax.random.fold_in(jax.random.fold_in(stream_key, 6), axis_at), (parts,), jnp.float32, low / len(split), high / len(split))
        loudness = loudness * jnp.repeat(jnp.exp(steps), shape[axis_at] // parts).reshape((-1,) + (1,) * (len(shape) - 1 - axis_at))
    return loudness


def shared_out(rng, own, number, rows, amount, top, most, skew):
    ranking = jax.random.permutation(rng, amount)
    heavy_load, ordinary = portions_of(amount, rows * top, most, skew, True), portions_of(amount, rows * top, most, skew, False)
    places = jnp.arange(amount)

    def named(tallies, rotation):
        used = int((tallies > 0).sum())
        fixed = max(1, used // 4)
        shifted = fixed + (places - fixed + rotation * (used - fixed)) % max(1, amount - fixed)
        return jnp.zeros((amount,), jnp.int32).at[ranking[jnp.where(places < fixed, places, shifted)]].set(jnp.asarray(tallies, jnp.int32))

    tallies = jnp.where(number % 4 == 0, named(heavy_load, number // 4), named(ordinary, number - number // 4 - 1))
    mixed = jax.random.permutation(jax.random.fold_in(own, 3), amount)
    donor, sink = mixed[0:amount // 2 * 2:2], mixed[1:amount // 2 * 2:2]
    room = jnp.minimum(tallies[donor] - 1, most - tallies[sink]) // 2
    room = jnp.where((donor == ranking[0]) | (sink == ranking[0]) | (tallies[sink] == 0), 0, jnp.maximum(room, 0))
    shifted = jax.random.randint(jax.random.fold_in(own, 4), (amount // 2,), 0, 1 << 20) % (room + 1)
    tallies = tallies.at[donor].add(-shifted).at[sink].add(shifted)
    labels = jnp.searchsorted(jnp.cumsum(tallies), jnp.arange(rows * top), side="right").astype(jnp.int32)
    listing = labels.reshape(top, rows).T
    listing = listing[jax.random.permutation(jax.random.fold_in(own, 1), rows)]
    rotation = jax.random.randint(jax.random.fold_in(own, 2), (rows, 1), 0, top)
    return jnp.take_along_axis(listing, (jnp.arange(top)[None, :] + rotation) % top, axis=1)


def portions_of(count, total, limit, lean, full):
    portions = [(1 << 20) // math.isqrt(rank ** lean) + 1 for rank in range(1, count + 1)]
    largest = limit if full else min(limit, max(-(-total // count), total * portions[0] // sum(portions)))
    least = 1 if total - largest >= count - 1 else 0
    counts, surplus = [largest] + [least] * (count - 1), total - largest - least * (count - 1)
    while surplus > 0:
        movable = [i for i in range(1, count) if counts[i] < largest] or [i for i in range(1, count) if counts[i] < limit]
        mass, budget = sum([portions[i] for i in movable]), surplus
        for i in movable:
            more = min(limit - counts[i], max(1, budget * portions[i] // mass), surplus)
            counts[i] = counts[i] + more
            surplus = surplus - more
    return np.array(counts)


def gaussian(rng, extent, spread, reach, pieces=(), kind=jnp.bfloat16):
    values = spread * jax.random.normal(rng, extent, jnp.float32)
    if pieces:
        values = values * shard_levels(rng, extent, pieces, -0.22, 0.18)
    return jnp.clip(values, -reach, reach).astype(kind)


def heavy_noise(rng, extent, spread, reach, cuts, heavy, held_as=jnp.bfloat16):
    result = spread * jax.random.normal(rng, extent, jnp.float32)
    if cuts:
        result = result * shard_levels(rng, extent, cuts, -0.22, 0.18)
    return jnp.clip(with_spikes(result, jax.random.fold_in(rng, 3), *heavy), -reach, reach).astype(held_as)


def setup_inputs(seed: int = 0) -> dict:
    arg_keys = jax.random.split(jax.random.key(seed), 11)
    tokens = heavy_noise(arg_keys[0], (TOKENS, D), 1.0, 6.0, ((0, 16),), (0, 1, 16, 2.0))
    cache = draw_cache(jax.random.fold_in(arg_keys[10], 71), 0)
    nb_row = place_ends(jax.random.randint(arg_keys[2], (STRETCHES, KN), 0, DB_DEV), jax.random.fold_in(arg_keys[2], 1), 0, DB_DEV - 1).astype(jnp.int32)
    nb_owner_keys = jax.random.split(jax.random.fold_in(arg_keys[3], 1), STRETCHES // STRETCH_DEV)
    nb_owner_turns = jax.random.permutation(jax.random.fold_in(arg_keys[3], 3), STRETCHES // STRETCH_DEV)
    nb_owner = jax.vmap(lambda own, number: shared_out(jax.random.fold_in(arg_keys[3], 2), own, number, STRETCH_DEV, N_DP, KN, CAP, 2))(nb_owner_keys, nb_owner_turns).reshape((STRETCHES, KN))
    nb_len = draw_nb_len(jax.random.fold_in(arg_keys[10], 71), 0)
    w_query = gaussian(arg_keys[5], (D, D), D ** -0.5, 0.09375, ((0, 16), (1, 8)))
    w_key = gaussian(arg_keys[6], (ENC, D), ENC ** -0.5, 0.1875, ((0, 16), (1, 8)))
    w_value = gaussian(arg_keys[7], (ENC, D), ENC ** -0.5, 0.1875, ((0, 16), (1, 8)))
    w_out = gaussian(arg_keys[8], (D, D), D ** -0.5, 0.09375, ((0, 8), (1, 16)))
    grad_out = heavy_noise(arg_keys[9], (TOKENS, D), 1.0, 6.0, ((0, 16),), (0, 1, 16, 2.0))
    return {"tokens": tokens, "cache": cache, "nb_row": nb_row, "nb_owner": nb_owner, "nb_len": nb_len, "w_query": w_query, "w_key": w_key, "w_value": w_value, "w_out": w_out, "grad_out": grad_out}


def group_heads(left_side, right_side, groups):
    span = left_side.shape[1] // groups
    summed = jnp.zeros((left_side.shape[0], right_side.shape[1]), jnp.float32)
    for group_index in range(groups):
        term = jnp.dot(left_side[:, group_index * span:(group_index + 1) * span], right_side[group_index * span:(group_index + 1) * span, :], preferred_element_type=jnp.float32).astype(jnp.bfloat16)
        term = lax.optimization_barrier(term)
        summed = summed + term.astype(jnp.float32)
    return summed

def group_rows(left_side, right_side, groups):
    span = left_side.shape[0] // groups
    summed = jnp.zeros((left_side.shape[1], right_side.shape[1]), jnp.float32)
    for group_index in range(groups):
        term = jnp.dot(left_side[group_index * span:(group_index + 1) * span].T, right_side[group_index * span:(group_index + 1) * span], preferred_element_type=jnp.float32).astype(jnp.bfloat16)
        term = lax.optimization_barrier(term)
        summed = summed + term.astype(jnp.float32)
    return summed

def one_stretch(stretch_item):
    query_block, key_block, value_block, key_valid, grad_block = stretch_item
    score_scale = HD ** (-0.5)
    query_wide = query_block.astype(jnp.float32)
    key_wide = key_block.astype(jnp.float32)
    value_wide = value_block.astype(jnp.float32)
    grad_wide = grad_block.astype(jnp.float32)
    scores = jnp.einsum('qhd,khd->hqk', query_wide, key_wide) * score_scale
    scores = jnp.where(key_valid[None, None, :], scores, -1e+30)
    row_top = lax.optimization_barrier(jnp.max(scores, axis=2, keepdims=True))
    weights_exp = jnp.exp(scores - row_top)
    prob_wide = weights_exp / lax.optimization_barrier(jnp.sum(weights_exp, axis=2, keepdims=True))
    prob = lax.optimization_barrier(prob_wide.astype(jnp.bfloat16)).astype(jnp.float32)
    attended = jnp.einsum('hqk,khd->qhd', prob, value_wide).astype(jnp.bfloat16)
    grad_prob = jnp.einsum('qhd,khd->hqk', grad_wide, value_wide)
    grad_values = jnp.einsum('hqk,qhd->khd', prob, grad_wide).astype(jnp.bfloat16)
    delta_rows = lax.optimization_barrier(jnp.sum(prob_wide * grad_prob, axis=2, keepdims=True))
    grad_scores = (prob_wide * (grad_prob - delta_rows) * score_scale).astype(jnp.bfloat16)
    grad_scores = lax.optimization_barrier(grad_scores).astype(jnp.float32)
    grad_queries = jnp.einsum('hqk,khd->qhd', grad_scores, key_wide).astype(jnp.bfloat16)
    grad_keys = jnp.einsum('hqk,qhd->khd', grad_scores, query_wide).astype(jnp.bfloat16)
    return (attended, grad_queries, grad_keys, grad_values)

def reference(tokens, cache, nb_row, nb_owner, nb_len, w_query, w_key, w_value, w_out, grad_out):
    wide_tokens = tokens.astype(jnp.float32)
    inv_rms = lax.rsqrt(lax.optimization_barrier(jnp.mean(wide_tokens * wide_tokens, axis=1, keepdims=True)) + 1e-06)
    normed_wide = wide_tokens * inv_rms
    normed = normed_wide.astype(jnp.bfloat16)
    queries = jnp.dot(normed, w_query, preferred_element_type=jnp.float32).astype(jnp.bfloat16)
    picked = (nb_owner * DB_DEV + nb_row).reshape(-1).astype(jnp.int32)
    blocks = jnp.take(cache, picked, axis=0)
    flat_blocks = blocks.reshape(STRETCHES * KN * NL, ENC)
    keys = jnp.dot(flat_blocks, w_key, preferred_element_type=jnp.float32).astype(jnp.bfloat16)
    values = jnp.dot(flat_blocks, w_value, preferred_element_type=jnp.float32).astype(jnp.bfloat16)
    grad_attn = jnp.dot(grad_out, w_out.T, preferred_element_type=jnp.float32).astype(jnp.bfloat16)
    positions = jnp.arange(NL, dtype=jnp.int32)
    key_valid = (positions[None, None, :] < nb_len[:, :, None]).reshape(STRETCHES, KN * NL)
    attended, grad_queries, grad_keys, grad_values = lax.map(one_stretch, (queries.reshape(STRETCHES, CL, HEADS, HD), keys.reshape(STRETCHES, KN * NL, HEADS, HD), values.reshape(STRETCHES, KN * NL, HEADS, HD), key_valid, grad_attn.reshape(STRETCHES, CL, HEADS, HD)))
    attended = attended.reshape(TOKENS, D)
    grad_queries = grad_queries.reshape(TOKENS, D)
    grad_keys = grad_keys.reshape(STRETCHES * KN * NL, D)
    grad_values = grad_values.reshape(STRETCHES * KN * NL, D)
    mixed = (wide_tokens + group_heads(attended, w_out, N_MP)).astype(jnp.bfloat16)
    grad_query = group_rows(normed, grad_queries, N_DP)
    grad_wout = group_rows(attended, grad_out, N_DP)
    grad_key = group_rows(flat_blocks, grad_keys, N_DP)
    grad_value = group_rows(flat_blocks, grad_values, N_DP)
    grad_normed = group_heads(grad_queries, w_query.T, N_MP)
    stat_rows = lax.optimization_barrier(jnp.mean(grad_normed * normed_wide, axis=1, keepdims=True))
    grad_tokens = (grad_out.astype(jnp.float32) + inv_rms * (grad_normed - normed_wide * stat_rows)).astype(jnp.bfloat16)
    return (mixed, grad_tokens, grad_query, grad_key, grad_value, grad_wout)
```

```python
import functools

import jax
import jax.numpy as jnp
from jax import lax
from jax.experimental import pallas as pl
from jax.experimental.pallas import tpu as pltpu
from jax.sharding import PartitionSpec as P

HD = 128
CL = 64
KN = 2
CAP = 3
SIDE = 4
bf16 = jnp.bfloat16
f32 = jnp.float32


def plane_pairs(dy, dx):
    pairs = []
    for s in range(SIDE * SIDE):
        y, x = divmod(s, SIDE)
        pairs.append((s, ((y + dy) % SIDE) * SIDE + (x + dx) % SIDE))
    return pairs


def column_pairs(dz, dc):
    pairs = []
    for s in range(2 * SIDE):
        z, c = divmod(s, 2)
        pairs.append((s, ((z + dz) % SIDE) * 2 + (c + dc) % 2))
    return pairs


def move_y(a, d):
    return lax.ppermute(a, "dp", plane_pairs(d, 0))


def move_x(a, d):
    return lax.ppermute(a, "dp", plane_pairs(0, d))


def move_z(a, d):
    return lax.ppermute(a, "mp", column_pairs(d, 0))


def swap_core(a):
    return lax.ppermute(a, "mp", column_pairs(0, 1))


def dot(a, b, dims):
    return lax.dot_general(a, b, (dims, ((), ())), preferred_element_type=f32)


NN = ((1,), (0,))
NT = ((1,), (1,))
TN = ((0,), (0,))


def gather_first(part, small):
    one, three, two = small(part, 1), small(part, -1), small(part, 2)
    return jnp.stack([part, one, two, three])


def gather_second(four, large):
    one, three = large(four, 1), large(four, -1)
    two_a = large(one[:2], 1)
    two_b = large(three[2:], -1)
    return four, one, two_a, two_b, three


def scatter_first(parts, large):
    zero, one, two_a, two_b, three = parts
    relay_a = large(two_a, -1)
    relay_b = large(two_b, 1)
    one = jnp.concatenate(
        [(one[:2].astype(f32) + relay_a.astype(f32)).astype(bf16), one[2:]]
    )
    three = jnp.concatenate(
        [three[:2], (three[2:].astype(f32) + relay_b.astype(f32)).astype(bf16)]
    )
    got_a, got_b = large(one, -1), large(three, 1)
    return [
        (zero[b].astype(f32) + got_a[b].astype(f32) + got_b[b].astype(f32))
        for b in range(SIDE)
    ]


def scatter_second(rows, small):
    one, two, three = (rows[b].astype(bf16) for b in (1, 2, 3))
    got = (small(one, -1), small(two, -2), small(three, 1))
    return rows[0] + got[0].astype(f32) + got[1].astype(f32) + got[2].astype(f32)


COUNTS = (4, 4, 2, 2, 4)
STARTS = (0, 4, 8, 10, 12)


def held(k, at, n):
    return jnp.clip(k - at, 0, n - 1)


def project_kernel(starts, counts, more, last, ids, x_ref, *refs):
    n = len(starts)
    parts, refs = refs[:n], refs[n:]
    if more:
        acc_in, side_in, refs = refs[0], refs[1], refs[2:]
    outs, (acc, side) = refs[:-2], refs[-2:]
    k = pl.program_id(0)

    @pl.when(k == 0)
    def _():
        if more:
            acc[...] = acc_in[...]
            side[...] = side_in[...]
        else:
            acc[...] = jnp.zeros_like(acc)
            side[...] = jnp.zeros_like(side)

    span = x_ref.shape[1]
    for at, count, part in zip(starts, counts, parts):

        @pl.when((k >= at) & (k < at + count))
        def _():
            acc[...] += dot(x_ref[...], part[0, :span, :], NN)
            tail = part.shape[1] - span
            row = pl.multiple_of(ids[k] * tail, 8)
            side[pl.ds(row, tail), :] = part[0, span:, :].astype(f32)

    @pl.when(k == pl.num_programs(0) - 1)
    def _():
        if last:
            outs[0][...] = acc[...]
            outs[1][...] = acc[...].astype(bf16)
            outs[2][...] = side[...].astype(bf16)
        else:
            outs[0][...] = acc[...]
            outs[1][...] = side[...]


def project(x, parts, ids, prev, last):
    tokens = x.shape[0]
    counts = tuple(p.shape[0] for p in parts)
    starts = tuple(sum(counts[:i]) for i in range(len(counts)))
    rows, cols = parts[0].shape[1:]
    span = x.shape[1] // (SIDE * SIDE)
    side_rows = (rows - span) * SIDE * SIDE
    specs = [pl.BlockSpec((tokens, span), lambda k, ids: (0, ids[k]))]
    for at, n in zip(starts, counts):
        specs.append(
            pl.BlockSpec((1, rows, cols), lambda k, ids, at=at, n=n: (held(k, at, n), 0, 0))
        )
    whole = lambda r: pl.BlockSpec((r, cols), lambda k, ids: (0, 0))
    if prev is not None:
        specs += [whole(tokens), whole(side_rows)]
    if last:
        shapes = [(tokens, f32), (tokens, bf16), (side_rows, bf16)]
    else:
        shapes = [(tokens, f32), (side_rows, f32)]
    steps = sum(counts)
    return pl.pallas_call(
        functools.partial(project_kernel, starts, counts, prev is not None, last),
        out_shape=[jax.ShapeDtypeStruct((r, cols), t) for r, t in shapes],
        grid_spec=pltpu.PrefetchScalarGridSpec(
            num_scalar_prefetch=1,
            grid=(steps,),
            in_specs=specs,
            out_specs=[whole(r) for r, _ in shapes],
            scratch_shapes=[pltpu.VMEM((tokens, cols), f32), pltpu.VMEM((side_rows, cols), f32)],
        ),
        cost_estimate=pl.CostEstimate(
            flops=2 * tokens * span * cols * steps,
            bytes_accessed=2 * steps * (tokens * span + rows * cols),
            transcendentals=0,
        ),
        name="project",
    )(ids, x, *parts, *(prev or ()))


def attend_kernel(
    lens, place, q_ref, g_ref, own_ref, other_ref, wk_ref, wv_ref,
    att_ref, gq_ref, gwk_ref, gwv_ref,
):
    c = pl.program_id(0)
    width = own_ref.shape[-1]
    piece = own_ref.shape[2]
    half = SIDE * KN * piece
    scale = HD ** (-0.5)
    block = jnp.concatenate(
        [own_ref[...].reshape(half, width), other_ref[...].reshape(half, width)], axis=0
    )
    keys = dot(block, wk_ref[...], NN).astype(bf16)
    values = dot(block, wv_ref[...], NN).astype(bf16)
    spot = lax.broadcasted_iota(jnp.int32, (1, 2 * half), 1)
    side = spot // half
    back = (spot // (KN * piece)) % SIDE
    which = (spot // piece) % KN
    z = (place[0] - back + SIDE) % SIDE
    core = jnp.where(side == 0, place[1], 1 - place[1])
    position = (z * 2 + core) * piece + spot % piece
    valid = position < jnp.where(which == 0, lens[c * KN], lens[c * KN + 1])
    grad_keys, grad_values = [], []
    for h in range(q_ref.shape[1] // HD):
        cols = slice(h * HD, (h + 1) * HD)
        q, g = q_ref[:, cols], g_ref[:, cols]
        kh, vh = keys[:, cols], values[:, cols]
        scores = jnp.where(valid, dot(q, kh, NT) * scale, -1e30)
        top = jnp.max(scores, axis=1, keepdims=True)
        e = jnp.exp(scores - top)
        prob_wide = e / jnp.sum(e, axis=1, keepdims=True)
        prob = prob_wide.astype(bf16)
        att_ref[:, cols] = dot(prob, vh, NN).astype(bf16)
        grad_prob = dot(g, vh, NT)
        delta = jnp.sum(prob_wide * grad_prob, axis=1, keepdims=True)
        grad_scores = (prob_wide * (grad_prob - delta) * scale).astype(bf16)
        gq_ref[:, cols] = dot(grad_scores, kh, NN).astype(bf16)
        grad_keys.append(dot(grad_scores, q, TN).astype(bf16))
        grad_values.append(dot(prob, g, TN).astype(bf16))
    gk = dot(block, jnp.concatenate(grad_keys, axis=1), TN)
    gv = dot(block, jnp.concatenate(grad_values, axis=1), TN)

    @pl.when(c == 0)
    def _():
        gwk_ref[...] = gk
        gwv_ref[...] = gv

    @pl.when(c > 0)
    def _():
        gwk_ref[...] += gk
        gwv_ref[...] += gv


def attend(lens, place, q, g, own, other, wk, wv):
    tokens, cols = q.shape
    steps = tokens // CL
    piece, width = own.shape[2:]
    rows = pl.BlockSpec((CL, cols), lambda c, *_: (c, 0))
    blocks = pl.BlockSpec((SIDE, KN, piece, width), lambda c, *_: (0, c, 0, 0))
    whole = pl.BlockSpec((width, cols), lambda c, *_: (0, 0))
    return pl.pallas_call(
        attend_kernel,
        out_shape=[
            jax.ShapeDtypeStruct((tokens, cols), bf16),
            jax.ShapeDtypeStruct((tokens, cols), bf16),
            jax.ShapeDtypeStruct((width, cols), f32),
            jax.ShapeDtypeStruct((width, cols), f32),
        ],
        grid_spec=pltpu.PrefetchScalarGridSpec(
            num_scalar_prefetch=2,
            grid=(steps,),
            in_specs=[rows, rows, blocks, blocks, whole, whole],
            out_specs=[rows, rows, whole, whole],
        ),
        cost_estimate=pl.CostEstimate(
            flops=8 * 2 * SIDE * KN * piece * width * cols * steps,
            bytes_accessed=8 * tokens * cols + 12 * width * cols,
            transcendentals=tokens * 256 * 4,
        ),
        name="attend",
    )(lens, place, q, g, own, other, wk, wv)


def weight_kernel(starts, counts, ids, x_ref, y_ref, side_ref, *outs):
    k = pl.program_id(0)
    span = x_ref.shape[0]
    for at, n, out in zip(starts, counts, outs):

        @pl.when((k >= at) & (k < at + n))
        def _():
            tail = out.shape[1] - span
            out[0, :span, :] = dot(x_ref[...], y_ref[...], NN).astype(bf16)
            row = pl.multiple_of(ids[k] * tail, 8)
            out[0, span:, :] = side_ref[pl.ds(row, tail), :].astype(bf16)


def weight_terms(xt, y, side, ids):
    width, tokens = xt.shape
    cols = y.shape[1]
    steps = SIDE * SIDE
    span = width // steps
    rows = span + side.shape[0] // steps
    out_specs = []
    for at, n in zip(STARTS, COUNTS):
        out_specs.append(
            pl.BlockSpec((1, rows, cols), lambda k, ids, at=at, n=n: (held(k, at, n), 0, 0))
        )
    return pl.pallas_call(
        functools.partial(weight_kernel, STARTS, COUNTS),
        out_shape=[jax.ShapeDtypeStruct((n, rows, cols), bf16) for n in COUNTS],
        grid_spec=pltpu.PrefetchScalarGridSpec(
            num_scalar_prefetch=1,
            grid=(steps,),
            in_specs=[
                pl.BlockSpec((span, tokens), lambda k, ids: (ids[k], 0)),
                pl.BlockSpec((tokens, cols), lambda k, ids: (0, 0)),
                pl.BlockSpec(side.shape, lambda k, ids: (0, 0)),
            ],
            out_specs=out_specs,
        ),
        cost_estimate=pl.CostEstimate(
            flops=2 * width * tokens * cols,
            bytes_accessed=2 * (width * tokens + tokens * cols + steps * rows * cols),
            transcendentals=0,
        ),
        name="weight_terms",
    )(ids, xt, y, side)


def head_kernel(starts, counts, where, y_ref, *refs):
    parts, out = refs[:-1], refs[-1]
    k = pl.program_id(0)
    span = out.shape[3]
    for at, n, part in zip(starts, counts, parts):

        @pl.when((k >= at) & (k < at + n))
        def _():
            out[0, 0] = dot(y_ref[...], part[0, :span, :], NT).astype(bf16)


def head_terms(y, parts, where):
    tokens, cols = y.shape
    rows = parts[0].shape[1]
    steps = SIDE * SIDE
    span = tokens // 2
    specs = [pl.BlockSpec((tokens, cols), lambda k, where: (0, 0))]
    for at, n in zip(STARTS, COUNTS):
        specs.append(
            pl.BlockSpec((1, rows, cols), lambda k, where, at=at, n=n: (held(k, at, n), 0, 0))
        )
    return pl.pallas_call(
        functools.partial(head_kernel, STARTS, COUNTS),
        out_shape=jax.ShapeDtypeStruct((2, SIDE, tokens, 2 * 256), bf16),
        grid_spec=pltpu.PrefetchScalarGridSpec(
            num_scalar_prefetch=1,
            grid=(steps,),
            in_specs=specs,
            out_specs=pl.BlockSpec(
                (1, 1, tokens, 256),
                lambda k, where: (where[k, 0], where[k, 1], 0, where[k, 2]),
            ),
        ),
        cost_estimate=pl.CostEstimate(
            flops=2 * tokens * cols * 256 * steps,
            bytes_accessed=2 * steps * (tokens * 256 + rows * cols),
            transcendentals=0,
        ),
        name="head_terms",
    )(where, y, *parts)


def scatter_heads(terms):
    got = swap_core(terms[1])
    mine = [terms[0, d].astype(f32) + got[d].astype(f32) for d in range(SIDE)]
    sent = [mine[d].astype(bf16) for d in range(1, SIDE)]
    back = (move_z(sent[0], 1), move_z(sent[1], 2), move_z(sent[2], -1))
    return mine[0] + back[0].astype(f32) + back[1].astype(f32) + back[2].astype(f32)


def on_device(tokens, cache, nb_row, nb_owner, nb_len, w_query, w_key, w_value, w_out, grad_out):
    dp_count = lax.axis_size("dp")
    dp_place = lax.axis_index("dp")
    mp_place = lax.axis_index("mp")
    y, x = dp_place // SIDE, dp_place % SIDE
    z, core = mp_place // 2, mp_place % 2
    tok_rows, width = tokens.shape
    request_count = nb_row.shape[0] * KN
    cache_rows, block_len, enc_width = cache.shape
    width_share = width // lax.axis_size("mp")
    piece = block_len // lax.axis_size("mp")

    first = jnp.arange(dp_count) // SIDE
    second = jnp.arange(dp_count) % SIDE
    ids_a = (((y - first) % SIDE) * SIDE + (x - second) % SIDE).astype(jnp.int32)
    ids_b = (((y - second) % SIDE) * SIDE + (x - first) % SIDE).astype(jnp.int32)

    def wanted_at(ids):
        return jnp.stack(
            [(ids // 2) % 2 ^ core, (ids // SIDE - z) % SIDE, ids % 2], axis=1
        ).astype(jnp.int32)

    four_a = gather_first(jnp.concatenate([w_query, w_key]), move_x)
    four_b = gather_first(jnp.concatenate([w_out.T, w_value]), move_y)

    owners = nb_owner.reshape(-1)
    wanted = nb_row.reshape(-1)
    req_order = jnp.arange(request_count)
    earlier = (owners[:, None] == owners[None, :]) & (req_order[None, :] < req_order[:, None])
    rank_seen = jnp.sum(earlier.astype(jnp.int32), axis=1)
    slot_of = owners * CAP + rank_seen
    slot_hits = (slot_of[:, None] == jnp.arange(dp_count * CAP)[None, :]).astype(jnp.int32)
    asked_ids = (jnp.sum(slot_hits * (wanted[:, None] + 1), axis=0) - 1).reshape(dp_count, CAP)
    picked_rows = jnp.clip(
        lax.all_to_all(asked_ids, "dp", split_axis=0, concat_axis=0, tiled=True), 0, cache_rows - 1
    )
    mine = lax.dynamic_slice_in_dim(cache, mp_place * piece, piece, 1)
    picked = mine.at[picked_rows.reshape(-1)].get(mode="promise_in_bounds")
    picked = picked.reshape(dp_count, CAP, piece, enc_width)
    arrived = lax.all_to_all(picked, "dp", split_axis=0, concat_axis=0, tiled=True)
    arrived = arrived.reshape(dp_count * CAP, piece, enc_width)
    own = arrived.at[slot_of].get(mode="promise_in_bounds")
    own = jnp.stack([own, move_z(own, 1), move_z(own, 2), move_z(own, -1)])
    other = swap_core(own)

    parts_a = gather_second(four_a, move_y)
    parts_b = gather_second(four_b, move_x)

    wide_tokens = tokens.astype(f32)
    inv_rms = lax.rsqrt(jnp.mean(wide_tokens * wide_tokens, axis=1, keepdims=True) + 1e-06)
    normed = (wide_tokens * inv_rms).astype(bf16)
    normed_t = normed.T
    grad_out_t = grad_out.T

    early = (0, 1, 4)
    late = (2, 3)

    def ids_of(ids, which):
        return jnp.concatenate([ids[STARTS[i] : STARTS[i] + COUNTS[i]] for i in which])

    def gathered_project(act, parts, ids):
        prev = project(act, [parts[i] for i in early], ids_of(ids, early), None, False)
        return project(act, [parts[i] for i in late], ids_of(ids, late), prev, True)

    queries_wide, queries, key_full = gathered_project(normed, parts_a, ids_a)
    _, grad_attn, value_full = gathered_project(grad_out, parts_b, ids_b)

    place = jnp.stack([z, core]).astype(jnp.int32)
    attended, grad_queries, grad_wk, grad_wv = attend(
        nb_len.reshape(-1), place, queries, grad_attn, own, other, key_full, value_full
    )

    rows_b = scatter_first(weight_terms(grad_out_t, attended, grad_wv, ids_b), move_x)
    rows_a = scatter_first(weight_terms(normed_t, grad_queries, grad_wk, ids_a), move_y)
    mixed_sum = scatter_heads(head_terms(attended, parts_b, wanted_at(ids_b)))
    stat = jnp.sum(grad_queries.astype(f32) * queries_wide, axis=1)
    stat = stat + swap_core(stat)
    stat = stat + move_z(stat, 1) + move_z(stat, 2) + move_z(stat, -1)
    grad_normed = scatter_heads(head_terms(grad_queries, parts_a, wanted_at(ids_a)))

    token_cols = lax.dynamic_slice_in_dim(tokens, mp_place * width_share, width_share, 1)
    token_cols = token_cols.astype(f32)
    mixed = (token_cols + mixed_sum).astype(bf16)
    out_cols = lax.dynamic_slice_in_dim(grad_out, mp_place * width_share, width_share, 1)
    normed_cols = token_cols * inv_rms
    grad_tokens = (
        out_cols.astype(f32) + inv_rms * (grad_normed - normed_cols * (stat / width)[:, None])
    ).astype(bf16)

    end_b = scatter_second(rows_b, move_y)
    end_a = scatter_second(rows_a, move_x)
    span = width // dp_count
    grad_query, grad_key = end_a[:span], end_a[span:]
    grad_wout, grad_value = end_b[:span].T, end_b[span:]
    return (mixed, grad_tokens, grad_query, grad_key, grad_value, grad_wout)


def solution(mesh):
    return jax.shard_map(
        on_device,
        mesh=mesh,
        in_specs=(
            P("dp", None),
            P("dp", None, None),
            P("dp", None),
            P("dp", None),
            P("dp", None),
            P("dp", "mp"),
            P("dp", "mp"),
            P("dp", "mp"),
            P("mp", "dp"),
            P("dp", None),
        ),
        out_specs=(
            P("dp", "mp"),
            P("dp", "mp"),
            P("dp", "mp"),
            P("dp", "mp"),
            P("dp", "mp"),
            P("mp", "dp"),
        ),
        check_vma=False,
    )
```
